32 devices in a mesh: group: 2 (over y), seq: 4 (over z), head: 4 (over x, core).
Axes of the slice: x: 2, y: 2, z: 4, core: 2. Of those that a mesh axis runs over, the one named last changes fastest.
Arguments:
- q_lin: bfloat16 [3072, 2048], P(('group', 'seq'), 'head'), parts along dimension 0, may hold values from -6 to 6
- k_lin: bfloat16 [3072, 2048], P(('group', 'seq'), 'head'), parts along dimension 0, may hold values from -6 to 6
- v_lin: bfloat16 [3072, 2048], P(('group', 'seq'), 'head'), parts along dimension 0, may hold values from -6 to 6
- q_soft: bfloat16 [3072, 2048], P(('group', 'seq'), 'head'), parts along dimension 0, may hold values from -5 to 5
- k_soft: bfloat16 [3072, 2048], P(('group', 'seq'), 'head'), parts along dimension 0, may hold values from -5 to 5
- v_soft: bfloat16 [3072, 2048], P(('group', 'seq'), 'head'), parts along dimension 0, may hold values from -6 to 6
- segment: int32 [3072], P(('group', 'seq')), parts along dimension 0, may hold values from 0 to 3, as said below
Outputs:
- mixed_lin: bfloat16 [3072, 2048], P(('group', 'seq'), 'head'), parts along dimension 0
- mixed_soft: bfloat16 [3072, 2048], P(('group', 'seq'), 'head'), parts along dimension 0
The draws below stay inside these ranges and needn't reach their ends.
There are 2 independent parts, one for each index of `group`. The reference program is written for one: setup_inputs(seed, part) draws one part's arguments, and reference() takes and returns one part's arrays. A program takes and returns all parts, laid end to end along the dimension named above; each array names one. Nothing has to cross between parts.
Inputs may be any that keep to these rules, and one draw needn't show every extreme that they name: `segment`: document numbers never fall along the list; each of the 4 documents has 1 to 960 tokens and one has exactly 960.
All inputs are finite; a program needn't handle non-finite values.
Results may differ from the reference program's by a relative error of at most 0.0075.
Values may be sent and summed in bfloat16 or wider, within the bound.
A program may use at most 128 MiB of HBM per device.

```python
import jax
import jax.numpy as jnp
from jax import lax

HEADS = 16
HEAD_DIM = 128
TOK_DEV = 384
NSEG = 4
TOKENS = 1536
SEG_MOST = 960


def drawn_rows(key, which):
    base = jnp.clip(jax.random.normal(jax.random.fold_in(key, which), (TOKENS, HEADS * HEAD_DIM), jnp.float32), -5.0, 5.0)
    return base


def draw_q_soft(key, part):
    return drawn_rows(key, 2).astype(jnp.bfloat16)


def draw_k_soft(key, part):
    return drawn_rows(key, 3).astype(jnp.bfloat16)


def draw_segment(key, part):
    remainder = TOKENS - SEG_MOST
    picks = jax.random.permutation(jax.random.fold_in(key, 5), remainder - 1)[:2] + 1
    cuts = jnp.sort(picks.astype(jnp.int32))
    shorter = jnp.stack([cuts[0], cuts[1] - cuts[0], remainder - cuts[1]]).astype(jnp.int32)
    longest_slot = jax.random.randint(jax.random.fold_in(key, 6), (), 0, NSEG, dtype=jnp.int32)
    slots = jnp.arange(NSEG, dtype=jnp.int32)
    source = jnp.clip(slots - (slots > longest_slot).astype(jnp.int32), 0, 2)
    lengths = jnp.where(slots == longest_slot, jnp.int32(SEG_MOST), shorter[source])
    ends = jnp.cumsum(lengths)[:-1]
    places = jnp.arange(TOKENS, dtype=jnp.int32)
    return jnp.sum((places[:, None] >= ends[None, :]).astype(jnp.int32), axis=1).astype(jnp.int32)


def levels(stream_key, extent, split, smallest, high):
    def one(dim, parts):
        draws = jax.random.uniform(jax.random.fold_in(jax.random.fold_in(stream_key, 6), dim), (parts,), jnp.float32, smallest / len(split), high / len(split))
        return jnp.repeat(jnp.exp(draws), extent[dim] // parts).reshape((-1,) + (1,) * (len(extent) - dim - 1))

    loudness = one(*split[0])
    for cut in split[1:]:
        loudness = loudness * one(*cut)
    return loudness


def normal_values(rng, dims, width, reach, split=(), kind=jnp.bfloat16):
    result = width * jax.random.normal(rng, dims, jnp.float32)
    if split:
        result = result * levels(rng, dims, split, -0.22, 0.18)
    return jnp.clip(result, -reach, reach).astype(kind)


def setup_inputs(seed: int = 0, part: int = 0) -> dict:
    streams_of = jax.random.split(jax.random.key(seed), 8)
    part_splits = jax.random.split(jax.random.fold_in(streams_of[7], part), 8)
    q_lin = normal_values(part_splits[0], (TOKENS, HEADS * HEAD_DIM), 1.0, 6.0, ((0, 4), (1, 4)))
    k_lin = normal_values(part_splits[1], (TOKENS, HEADS * HEAD_DIM), 1.0, 6.0, ((0, 4), (1, 4)))
    v_lin = normal_values(part_splits[2], (TOKENS, HEADS * HEAD_DIM), 1.0, 6.0, ((0, 4), (1, 4)))
    q_soft = draw_q_soft(jax.random.fold_in(jax.random.fold_in(streams_of[7], part), 71), part)
    k_soft = draw_k_soft(jax.random.fold_in(jax.random.fold_in(streams_of[7], part), 71), part)
    v_soft = normal_values(part_splits[5], (TOKENS, HEADS * HEAD_DIM), 1.0, 6.0, ((0, 4), (1, 4)))
    segment = draw_segment(jax.random.fold_in(jax.random.fold_in(streams_of[7], part), 71), part)
    return {"q_lin": q_lin, "k_lin": k_lin, "v_lin": v_lin, "q_soft": q_soft, "k_soft": k_soft, "v_soft": v_soft, "segment": segment}


def linear_layer(q_lin, k_lin, v_lin, segment):
    blocks = q_lin.shape[0] // TOK_DEV
    shape = (blocks, TOK_DEV, HEADS, HEAD_DIM)
    q_all = q_lin.reshape(shape)
    k_all = k_lin.reshape(shape)
    v_all = v_lin.reshape(shape)
    s_all = segment.reshape(blocks, TOK_DEV)
    places = jnp.arange(TOK_DEV, dtype=jnp.int32)

    def step(carry, inputs):
        memory_state, last_id = carry
        query_block_slice, key_block_slice, value_block_slice, s_blk = inputs
        scores = jnp.einsum('thd,shd->hts', query_block_slice, key_block_slice, preferred_element_type=jnp.float32)
        same = (s_blk[:, None] == s_blk[None, :]) & (places[:, None] >= places[None, :])
        scores = jnp.where(same[None], scores, 0.0)
        inner = jnp.einsum('hts,shd->thd', scores, value_block_slice.astype(jnp.float32), precision=lax.Precision.HIGHEST)
        apply = (s_blk.astype(jnp.float32) == last_id).astype(jnp.float32)
        outer_product = jnp.einsum('upi,pis->ups', query_block_slice.astype(jnp.float32), memory_state, precision=lax.Precision.HIGHEST)
        raw = inner + outer_product * apply[:, None, None]
        new_last = s_blk[-1].astype(jnp.float32)
        retain_mask = (s_blk == s_blk[-1]).astype(key_block_slice.dtype)
        local_state = jnp.einsum('piy,piw->iyw', key_block_slice * retain_mask[:, None, None], value_block_slice, preferred_element_type=jnp.float32)
        memory_state = jnp.where(last_id == new_last, memory_state, 0.0) + local_state
        normed = raw * lax.rsqrt(lax.optimization_barrier(jnp.mean(raw * raw, axis=-1, keepdims=True)) + 1e-06)
        return ((memory_state, new_last), normed.astype(jnp.bfloat16))
    start = (jnp.zeros((HEADS, HEAD_DIM, HEAD_DIM), jnp.float32), jnp.float32(-1.0))
    _, outs = lax.scan(step, start, (q_all, k_all, v_all, s_all))
    return outs.reshape(q_lin.shape)

def softmax_layer(q_soft, k_soft, v_soft, segment):
    total_rows = q_soft.shape[0]
    blocks = total_rows // TOK_DEV
    q_heads = q_soft.reshape(blocks, TOK_DEV, HEADS, HEAD_DIM).transpose(2, 0, 1, 3)
    k_heads = k_soft.reshape(total_rows, HEADS, HEAD_DIM).transpose(1, 0, 2)
    v_heads = v_soft.reshape(total_rows, HEADS, HEAD_DIM).transpose(1, 0, 2)
    key_pos = jnp.arange(total_rows, dtype=jnp.int32)
    q_pos_all = key_pos.reshape(blocks, TOK_DEV)
    q_seg_all = segment.reshape(blocks, TOK_DEV)
    scale = HEAD_DIM ** (-0.5)

    def per_head(inputs):
        q_head, k_head, v_head = inputs

        def per_block(block_in):
            query_block_slice, q_pos, q_seg = block_in
            scores = jnp.dot(query_block_slice, k_head.T, preferred_element_type=jnp.float32) * scale
            mask = (key_pos[None, :] <= q_pos[:, None]) & (segment[None, :] == q_seg[:, None])
            top = lax.optimization_barrier(jnp.max(jnp.where(mask, scores, -1e+30), axis=-1, keepdims=True))
            expo = jnp.where(mask, jnp.exp(scores - top), 0.0)
            total = lax.optimization_barrier(jnp.sum(expo, axis=-1, keepdims=True))
            summed = jnp.dot(expo.astype(jnp.bfloat16), v_head, preferred_element_type=jnp.float32)
            return (summed / total).astype(jnp.bfloat16)
        return lax.map(per_block, (q_head, q_pos_all, q_seg_all))
    outs = lax.map(per_head, (q_heads, k_heads, v_heads))
    return outs.transpose(1, 2, 0, 3).reshape(total_rows, HEADS * HEAD_DIM)

def reference(q_lin, k_lin, v_lin, q_soft, k_soft, v_soft, segment):
    mixed_lin = linear_layer(q_lin, k_lin, v_lin, segment)
    mixed_soft = softmax_layer(q_soft, k_soft, v_soft, segment)
    return (mixed_lin, mixed_soft)
```

```python
import functools

import jax
import jax.numpy as jnp
from jax import lax
from jax.experimental import pallas as pl
from jax.experimental.pallas import tpu as pltpu
from jax.sharding import PartitionSpec as P

HEAD_DIM = 128
HIDDEN = -1e30
MESH = pl.DeviceIdType.MESH


def across(a, b):
    return lax.dot_general(a, b, (((1,), (1,)), ((), ())), preferred_element_type=jnp.float32)


def kernel(n, heads, reach, last_rows, q_lin, k_lin, v_lin, q_soft, k_soft, v_soft, seg,
           out_lin, out_soft, kbuf, vbuf, segbuf, state_in, state_out, bias, column, raw, top, total, accum,
           k_send, k_recv, v_send, v_recv, seg_send, seg_recv, state_send, state_recv):
    rows = q_lin.shape[0]
    me = lax.axis_index("seq")
    right, left = lax.rem(me + 1, n), lax.rem(me + n - 1, n)
    scale = HEAD_DIM ** (-0.5)

    def cols(h):
        return pl.ds(pl.multiple_of(h * HEAD_DIM, HEAD_DIM), HEAD_DIM)

    def first_row(d):
        return rows - last_rows if d == reach else 0

    def move(own, buf, send, recv, d, h):
        at = pl.ds(first_row(d), rows - first_row(d))
        source = own.at[at, cols(h)] if d == 1 else buf.at[d - 2, h, at, :]
        return pltpu.make_async_remote_copy(
            src_ref=source, dst_ref=buf.at[d - 1, h, at, :], send_sem=send.at[d - 1, h],
            recv_sem=recv.at[d - 1, h], device_id={"seq": right}, device_id_type=MESH)

    def key_move(d, h):
        return move(k_soft, kbuf, k_send, k_recv, d, h)

    def value_move(d, h):
        return move(v_soft, vbuf, v_send, v_recv, d, h)

    def seg_move(d):
        return pltpu.make_async_remote_copy(
            src_ref=seg if d == 1 else segbuf.at[d - 2], dst_ref=segbuf.at[d - 1], send_sem=seg_send.at[d - 1],
            recv_sem=seg_recv.at[d - 1], device_id={"seq": right}, device_id_type=MESH)

    def state_move():
        return pltpu.make_async_remote_copy(
            src_ref=state_out, dst_ref=state_in, send_sem=state_send,
            recv_sem=state_recv, device_id={"seq": right}, device_id_type=MESH)

    barrier = pltpu.get_barrier_semaphore()
    for neighbour in (left, right):
        pl.semaphore_signal(barrier, inc=1, device_id={"seq": neighbour}, device_id_type=MESH)
    pl.semaphore_wait(barrier, 2)

    @pl.when(me < n - 1)
    def _():
        seg_move(1).start()
        for h in range(heads):
            key_move(1, h).start()
            value_move(1, h).start()

    own_row = seg[...].astype(jnp.float32)
    column[...] = jnp.transpose(jnp.broadcast_to(own_row, (HEAD_DIM, rows)))
    own_last = own_row[:, rows - 1:]
    query = lax.broadcasted_iota(jnp.int32, (rows, rows), 0)
    key = lax.broadcasted_iota(jnp.int32, (rows, rows), 1)
    bias[...] = jnp.where((column[:, :1] == own_row) & (key <= query), 0.0, HIDDEN)

    def local(h, _):
        at = cols(h)
        scores = across(q_lin[:, at], k_lin[:, at])
        scores = jnp.where(bias[...] == 0.0, scores, 0.0).astype(jnp.bfloat16)
        raw[h] = jnp.dot(scores, v_lin[:, at], preferred_element_type=jnp.float32)
        logits = across(q_soft[:, at], k_soft[:, at]) * scale + bias[...]
        peak = jnp.max(logits, axis=-1, keepdims=True)
        expo = jnp.exp(logits - peak)
        top[h] = jnp.broadcast_to(peak, (rows, HEAD_DIM))
        total[h] = jnp.broadcast_to(jnp.sum(expo, axis=-1, keepdims=True), (rows, HEAD_DIM))
        accum[h] = jnp.dot(expo.astype(jnp.bfloat16), v_soft[:, at], preferred_element_type=jnp.float32)
        return 0

    lax.fori_loop(0, heads, local, 0)

    for d in range(1, reach + 1):
        begin = first_row(d)

        @pl.when(me >= d)
        def _(d=d, begin=begin):
            seg_move(d).wait_recv()
            if d < reach:
                @pl.when(me < n - 1)
                def _():
                    seg_move(d + 1).start()
            theirs = segbuf[d - 1].astype(jnp.float32)
            bias[...] = jnp.where(column[:, :1] == theirs, 0.0, HIDDEN)

            def block(h, _):
                key_move(d, h).wait_recv()
                if d < reach:
                    @pl.when(me < n - 1)
                    def _():
                        key_move(d + 1, h).start()
                value_move(d, h).wait_recv()
                if d < reach:
                    @pl.when(me < n - 1)
                    def _():
                        value_move(d + 1, h).start()
                at = cols(h)
                logits = across(q_soft[:, at], kbuf[d - 1, h, begin:, :]) * scale + bias[:, begin:]
                before = top[h]
                peak = jnp.maximum(before, jnp.max(logits, axis=-1, keepdims=True))
                factor = jnp.exp(before - peak)
                expo = jnp.exp(logits - peak[:, :1])
                top[h] = peak
                total[h] = total[h] * factor + jnp.sum(expo, axis=-1, keepdims=True)
                accum[h] = accum[h] * factor + jnp.dot(
                    expo.astype(jnp.bfloat16), vbuf[d - 1, h, begin:, :], preferred_element_type=jnp.float32)
                return 0

            lax.fori_loop(0, heads, block, 0)

    keep = jnp.where(column[...] == own_last, 1.0, 0.0)

    @pl.when(me == 0)
    def _():
        state_in[...] = jnp.zeros_like(state_in)
        segbuf[0] = jnp.full((1, rows), -1, jnp.int32)

    @pl.when(me > 0)
    def _():
        state_move().wait_recv()

    before_last = segbuf[0].astype(jnp.float32)[:, rows - 1:]

    @pl.when(me < n - 1)
    def _():
        going = jnp.where(before_last == own_last, 1.0, 0.0)
        for h in range(heads):
            at = cols(h)
            kept = (k_lin[:, at].astype(jnp.float32) * keep).astype(jnp.bfloat16)
            own = lax.dot_general(
                kept, v_lin[:, at], (((0,), (0,)), ((), ())), preferred_element_type=jnp.float32)
            state_out[h] = (own + going * state_in[h].astype(jnp.float32)).astype(jnp.bfloat16)
        state_move().start()

    apply = jnp.where(column[...] == before_last, 1.0, 0.0)
    for h in range(heads):
        at = cols(h)
        outer = jnp.dot(q_lin[:, at], state_in[h], preferred_element_type=jnp.float32)
        mixed = raw[h] + outer * apply
        norm = lax.rsqrt(jnp.mean(mixed * mixed, axis=-1, keepdims=True) + 1e-6)
        out_lin[:, at] = (mixed * norm).astype(jnp.bfloat16)
        out_soft[:, at] = (accum[h] / total[h]).astype(jnp.bfloat16)

    for d in range(1, reach + 1):
        @pl.when((me >= d - 1) & (me < n - 1))
        def _(d=d):
            seg_move(d).wait_send()

            def sent(h, _):
                key_move(d, h).wait_send()
                value_move(d, h).wait_send()
                return 0

            lax.fori_loop(0, heads, sent, 0)

    @pl.when(me < n - 1)
    def _():
        state_move().wait_send()


def solution(mesh):
    n = mesh.shape["seq"]

    def on_device(q_lin, k_lin, v_lin, q_soft, k_soft, v_soft, segment):
        rows, width = q_lin.shape
        heads = width // HEAD_DIM
        longest = rows * n * 5 // 8
        reach = min(n - 1, (longest - 2) // rows + 1)
        last_rows = min(rows, -(-(longest - 1 - (reach - 1) * rows) // 128) * 128)
        vmem = pl.BlockSpec(memory_space=pltpu.VMEM)
        dma = pltpu.SemaphoreType.DMA
        out = jax.ShapeDtypeStruct((rows, width), jnp.bfloat16)
        blocks = (heads, rows, HEAD_DIM)
        return pl.pallas_call(
            functools.partial(kernel, n, heads, reach, last_rows),
            out_shape=(out, out),
            in_specs=[vmem] * 7,
            out_specs=(vmem, vmem),
            scratch_shapes=[
                pltpu.VMEM((reach,) + blocks, jnp.bfloat16),
                pltpu.VMEM((reach,) + blocks, jnp.bfloat16),
                pltpu.VMEM((reach, 1, rows), jnp.int32),
                pltpu.VMEM((heads, HEAD_DIM, HEAD_DIM), jnp.bfloat16),
                pltpu.VMEM((heads, HEAD_DIM, HEAD_DIM), jnp.bfloat16),
                pltpu.VMEM((rows, rows), jnp.float32),
                pltpu.VMEM((rows, HEAD_DIM), jnp.float32),
                pltpu.VMEM(blocks, jnp.float32),
                pltpu.VMEM(blocks, jnp.float32),
                pltpu.VMEM(blocks, jnp.float32),
                pltpu.VMEM(blocks, jnp.float32),
                dma((reach, heads)), dma((reach, heads)), dma((reach, heads)), dma((reach, heads)),
                dma((reach,)), dma((reach,)), dma, dma,
            ],
            compiler_params=pltpu.CompilerParams(
                collective_id=0, has_side_effects=True, vmem_limit_bytes=56 * 1024 * 1024),
        )(q_lin, k_lin, v_lin, q_soft, k_soft, v_soft, segment.reshape(1, rows))

    tokens = P(("group", "seq"), "head")
    return jax.shard_map(
        on_device, mesh=mesh, in_specs=(tokens,) * 6 + (P(("group", "seq")),),
        out_specs=(tokens, tokens), check_vma=False)
```
